32 devices in a mesh: dp: 8 (over y, x, core), mp: 4 (over z).
Axes of the slice: x: 2, y: 2, z: 4, core: 2. Of those that a mesh axis runs over, the one named last changes fastest.
Arguments:
- tokens: bfloat16 [2048, 3072], P('dp'), may hold values from -16 to 16
- weight: bfloat16 [3072, 3072], P(None, 'mp'), may hold values from -0.109375 to 0.109375
- norm_gain: float32 [128], replicated, may hold values from 0.1 to 1.9
- upstream: bfloat16 [2048, 3072], P('dp', 'mp'), may hold values from -0.176776695 to 0.176776695
Outputs:
- perturbation: float32 [3072, 3072], P('dp', 'mp')
- sharp_grad: float32 [3072, 3072], P('dp', 'mp')
The draws below stay inside these ranges and needn't reach their ends.
All inputs are finite; a program needn't handle non-finite values.
Results may differ from the reference program's by a relative error of at most 0.0028.
Values may be sent and summed in bfloat16 or wider, within the bound.
A program may use at most 64 MiB of HBM per device.

```python
import math
import jax
import jax.numpy as jnp
from jax import lax

FEAT = 3072
HEADS = 24
HEAD_DIM = 128
TOK_DEV = 256
TOKENS = 2048
N_DP = 8


def draw_tokens(key, part):
    key_values = jax.random.fold_in(key, 0)
    key_feature = jax.random.fold_in(key, 1)
    key_offset = jax.random.fold_in(key, 3)
    ramp = 0.5 + jnp.arange(FEAT, dtype=jnp.float32) / FEAT
    spread = jnp.exp(jax.random.uniform(key_feature, (FEAT,), jnp.float32, -1.15, 1.15))
    offset = 0.5 * jax.random.normal(key_offset, (1, FEAT), jnp.float32)
    values = jax.random.normal(key_values, (TOKENS, FEAT), jnp.float32) + offset
    return jnp.clip(values * ramp * spread, -16.0, 16.0).astype(jnp.bfloat16)


def draw_upstream(key, part):
    key_noise, key_pattern = jax.random.split(key)
    columns = HEADS * HEAD_DIM
    scale = TOKENS ** (-0.5)
    noise = jax.random.normal(key_noise, (TOKENS, columns), jnp.float32)
    amplitude = (5.0 / TOKENS) ** 0.5
    pattern = amplitude * jax.random.normal(key_pattern, (1, columns), jnp.float32)
    values = (noise + pattern) * scale
    return jnp.clip(values, -8.0 * scale, 8.0 * scale).astype(jnp.bfloat16)


def steps_of(own_key, extent, cuts, smallest, high):
    gain = 1.0
    for axis_at, parts in cuts:
        draws = jax.random.uniform(jax.random.fold_in(jax.random.fold_in(own_key, 6), axis_at), (parts,), jnp.float32, smallest / len(cuts), high / len(cuts))
        gain = gain * jnp.repeat(jnp.exp(draws), extent[axis_at] // parts).reshape((-1,) + (1,) * (len(extent) - 1 - axis_at))
    return gain


def bell_draw(own_key, dims, width, most, pieces=(), held_as=jnp.bfloat16):
    entries = jax.random.normal(own_key, dims, jnp.float32) * width
    if len(pieces) > 0:
        entries = steps_of(own_key, dims, pieces, -0.22, 0.18) * entries
    return jnp.clip(entries, min=-most, max=most).astype(held_as)


def setup_inputs(seed: int = 0) -> dict:
    keys = jax.random.split(jax.random.key(seed), 5)
    tokens = draw_tokens(jax.random.fold_in(keys[4], 71), 0)
    weight = bell_draw(keys[1], (FEAT, HEADS * HEAD_DIM), FEAT ** -0.5, 0.109375, ((1, 4),))
    norm_gain = jnp.clip(1.0 + 0.18 * jax.random.normal(keys[2], (HEAD_DIM,), jnp.float32), 0.1, 1.9)
    upstream = draw_upstream(jax.random.fold_in(keys[4], 71), 0)
    return dict(tokens=tokens, weight=weight, norm_gain=norm_gain, upstream=upstream)


radius_coef = 0.004

def head_backward(queries, upstream, norm_gain):
    count = queries.shape[0]
    grouped = queries.reshape(count, -1, HEAD_DIM)
    centred = grouped - lax.optimization_barrier(jnp.mean(grouped, axis=-1, keepdims=True))
    inverse = lax.rsqrt(lax.optimization_barrier(jnp.mean(centred * centred, axis=-1, keepdims=True)) + 1e-06)
    normed = centred * inverse
    scaled = upstream.astype(jnp.float32).reshape(count, -1, HEAD_DIM) * norm_gain
    result = (scaled - lax.optimization_barrier(jnp.mean(scaled, axis=-1, keepdims=True)) - normed * lax.optimization_barrier(jnp.mean(scaled * normed, axis=-1, keepdims=True))) * inverse
    return result.reshape(count, -1).astype(jnp.bfloat16)

def left_product(left, right):
    return lax.dot_general(left, right, (((0,), (0,)), ((), ())), preferred_element_type=jnp.float32)

def reference(tokens, weight, norm_gain, upstream):
    columns = HEADS * HEAD_DIM
    blocks = tokens.reshape(N_DP, TOK_DEV, FEAT)
    upper = upstream.reshape(N_DP, TOK_DEV, columns)

    def accumulate(carry, pair):
        block, grad_up = pair
        first = jnp.dot(block, weight, preferred_element_type=jnp.float32)
        first_grad = head_backward(first, grad_up, norm_gain)
        partial_sum = left_product(block, first_grad).astype(jnp.bfloat16)
        partial_sum = lax.optimization_barrier(partial_sum)
        return (carry + partial_sum.astype(jnp.float32), None)
    ascent, unused = lax.scan(accumulate, jnp.zeros((FEAT, columns), jnp.float32), (blocks, upper))
    total = jnp.sum(ascent * ascent)
    radius = radius_coef * math.sqrt(FEAT * columns)
    perturbation = ascent * (radius / (jnp.sqrt(total) + 1e-12))
    perturbed = (weight.astype(jnp.float32) + perturbation).astype(jnp.bfloat16)
    second = jnp.dot(tokens, perturbed, preferred_element_type=jnp.float32)
    second_grad = head_backward(second, upstream, norm_gain)
    sharp_grad = left_product(tokens, second_grad)
    return (perturbation, sharp_grad)
```

```python
import functools
import math

import jax
import jax.numpy as jnp
from jax import lax
from jax.experimental import pallas as pl
from jax.experimental.pallas import tpu as pltpu
from jax.sharding import PartitionSpec as P

radius_coef = 0.004
DIRECT = 128
F32 = jnp.float32
BF16 = jnp.bfloat16
MESH = pl.DeviceIdType.MESH


def head_backward(queries, upstream, norm_gain):
    head_dim = norm_gain.shape[0]
    count = queries.shape[0]
    grouped = queries.reshape(count, -1, head_dim)
    centred = grouped - jnp.mean(grouped, axis=-1, keepdims=True)
    inverse = lax.rsqrt(jnp.mean(centred * centred, axis=-1, keepdims=True) + 1e-06)
    normed = centred * inverse
    scaled = upstream.astype(jnp.float32).reshape(count, -1, head_dim) * norm_gain
    result = (
        scaled
        - jnp.mean(scaled, axis=-1, keepdims=True)
        - normed * jnp.mean(scaled * normed, axis=-1, keepdims=True)
    ) * inverse
    return result.reshape(count, -1).astype(jnp.bfloat16)


def left_product(left, right):
    return lax.dot_general(
        left, right, (((0,), (0,)), ((), ())), preferred_element_type=jnp.float32
    )


def general_step(tokens, weight, norm_gain, upstream):
    rows_own = weight.shape[0] // lax.axis_size("dp")
    radius = radius_coef * math.sqrt(weight.shape[0] * weight.shape[1] * lax.axis_size("mp"))
    row_start = lax.axis_index("dp") * rows_own
    first = jnp.dot(tokens, weight, preferred_element_type=jnp.float32)
    first_grad = head_backward(first, upstream, norm_gain)
    rounded = left_product(tokens, first_grad).astype(jnp.bfloat16)
    rounded = lax.optimization_barrier(rounded)
    owned = lax.psum_scatter(rounded.astype(jnp.float32), "dp", scatter_dimension=0, tiled=True)
    local_total = jnp.sum(owned * owned)
    total = lax.psum(local_total, ("dp", "mp"))
    perturbation = owned * (radius / (jnp.sqrt(total) + 1e-12))
    own_weight = lax.dynamic_slice_in_dim(weight, row_start, rows_own, 0)
    own_perturbed = (own_weight.astype(jnp.float32) + perturbation).astype(jnp.bfloat16)
    second = jnp.dot(
        tokens,
        lax.all_gather(own_perturbed, "dp", axis=0, tiled=True),
        preferred_element_type=jnp.float32,
    )
    second_grad = head_backward(second, upstream, norm_gain)
    sharp_grad = lax.psum_scatter(
        left_product(tokens, second_grad), "dp", scatter_dimension=0, tiled=True
    )
    return (perturbation, sharp_grad)


def cube_kernel(
    radius, n_mp,
    tok_ref, w_hbm, gain_ref, up_ref,
    pert_ref, sharp_ref,
    weight, query, near, side, turned, grads, grads2,
    part_out, part_in, moved, core_out, core_in, side_out, side_in, delta,
    sharp_out, sharp_in, total_dp, total_mp,
    load_sem, near_sem, send_sem, recv_sem,
):
    n_tok = tok_ref.shape[0]
    rows = pert_ref.shape[0]
    parts, head_dim = grads.shape[1], grads.shape[3]
    me = lax.axis_index("dp")
    z = lax.axis_index("mp")
    y, x, c = me // 4, (me // 2) % 2, me % 2
    oy, ox, oc = 1 - y, 1 - x, 1 - c

    def at(yy, xx, cc):
        return (yy * 2 + xx) * 2 + cc

    partner, x_peer, y_peer = at(y, x, oc), at(y, ox, c), at(oy, x, c)
    x_cross, y_cross = at(y, ox, oc), at(oy, x, oc)
    diagonal, far = at(oy, ox, c), at(oy, ox, oc)
    dp_peers = [partner, x_peer, y_peer, x_cross, y_cross, diagonal, far]
    mp_peers = [lax.rem(z + k, n_mp) for k in range(1, n_mp)]
    parity = z % 2
    z_pair = z + 1 - 2 * parity

    barrier = pltpu.get_barrier_semaphore()
    for peer in dp_peers:
        pl.semaphore_signal(barrier, inc=1, device_id={"dp": peer}, device_id_type=MESH)
    for peer in mp_peers:
        pl.semaphore_signal(barrier, inc=1, device_id={"mp": peer}, device_id_type=MESH)

    gather_peer = [x_peer, y_peer]
    reduce_peer = [y_peer, x_peer]

    def columns(s, k):
        return pl.ds((2 * k + s) * head_dim, head_dim)

    def features(owner):
        return pl.ds(pl.multiple_of(owner * rows, rows), rows)

    def block(index, size):
        return pl.ds(index * size, size)

    loads = []
    for k in range(parts):
        span = block(k, 2 * head_dim)
        loads.append(
            pltpu.make_async_copy(w_hbm.at[:, span], weight.at[:, span], load_sem.at[k])
        )
        loads[-1].start()
    near_copies = []
    for index, owner in enumerate([y_peer, me, x_peer]):
        near_copies.append(
            pltpu.make_async_copy(
                tok_ref.at[:, features(owner)], near.at[0, :, block(index, rows)],
                near_sem.at[index],
            )
        )
        near_copies[-1].start()

    started = []

    def send(source, target, device):
        index = len(started)
        copy = pltpu.make_async_remote_copy(
            src_ref=source, dst_ref=target,
            send_sem=send_sem.at[index], recv_sem=recv_sem.at[index],
            device_id=device, device_id_type=MESH,
        )
        copy.start()
        started.append(copy)
        return copy

    pl.semaphore_wait(barrier, len(dp_peers) + len(mp_peers))
    passed_rows = n_tok - DIRECT
    share = pl.ds(pl.multiple_of(parity * passed_rows, 16), DIRECT)
    passing = pl.ds(pl.multiple_of(parity * DIRECT, 16), passed_rows)
    brought = {}

    def bring(s, own):
        for twin in range(2):
            cc = oc if twin else c
            if s == 0:
                receiver, owner = at(y, ox, cc), at(y if own else oy, ox, cc)
                slot = 1 if own else 0
            else:
                receiver, owner = at(oy, x, cc), at(oy, x if own else ox, cc)
                slot = 0 if own else 1
            brought[s, own, twin] = (
                send(
                    tok_ref.at[share, features(owner)],
                    side.at[s, twin, share, block(slot, rows)], {"dp": receiver},
                ),
                slot,
            )

    bring(0, False)
    bring(1, False)
    from_partner = []
    for index, owner in enumerate([at(oy, x, oc), partner, at(y, ox, oc)]):
        from_partner.append(
            send(tok_ref.at[:, features(owner)], near.at[1, :, block(index, rows)], {"dp": partner})
        )
    bring(0, True)
    bring(1, True)
    passed = {}

    def pass_on(own):
        for s in range(2):
            for twin in range(2):
                copy, slot = brought[s, own, twin]
                copy.wait_recv()
                piece = side.at[s, twin, passing, block(slot, rows)]
                passed[s, own, twin] = send(piece, piece, {"mp": z_pair})

    def backward(out, s, k):
        half = n_tok // 2
        for low in (0, half):
            span = pl.ds(low, half)
            values = query[span, columns(s, k)]
            centred = values - jnp.mean(values, axis=-1, keepdims=True)
            inverse = lax.rsqrt(jnp.mean(centred * centred, axis=-1, keepdims=True) + 1e-06)
            normed = centred * inverse
            scaled = up_ref[span, columns(s, k)].astype(F32) * gain_ref[...]
            result = (
                scaled
                - jnp.mean(scaled, axis=-1, keepdims=True)
                - normed * jnp.mean(scaled * normed, axis=-1, keepdims=True)
            ) * inverse
            out[s, k, span] = result.astype(BF16)

    def spread(buffer, s, k):
        backward(buffer, s, k)
        own = buffer.at[s, k, block(0, n_tok)]
        far_copy = send(own, buffer.at[s, k, block(2, n_tok)], {"dp": gather_peer[s]})
        near_copy = send(own, buffer.at[s, k, block(1, n_tok)], {"dp": partner})
        return far_copy, near_copy

    def forward(buffer, s, k, copies):
        copies[0].wait_recv()
        return send(
            buffer.at[s, k, block(2, n_tok)], buffer.at[s, k, block(3, n_tok)], {"dp": partner}
        )

    gathers = {}
    for k in range(parts):
        loads[k].wait()
        span = block(k, 2 * head_dim)
        query[:, span] = jnp.dot(tok_ref[...], weight[:, span], preferred_element_type=F32)
        for s in range(2):
            gathers[s, k] = spread(grads, s, k)
    pass_on(False)

    for copy in near_copies:
        copy.wait()

    def turn_near(which):
        for index, places in enumerate([[(0, 0)], [(0, 1), (1, 1)], [(1, 0)]]):
            value = near[which, :, block(index, rows)].T
            for s, target in places:
                turned[s, target, :, block(which, n_tok)] = value

    def turn_side(s, own):
        for twin in range(2):
            passed[s, own, twin].wait_recv()
            slot = brought[s, own, twin][1]
            value = side[s, twin, :, block(slot, rows)].T
            turned[s, 1 if own else 0, :, block(2 + twin, n_tok)] = value

    turn_near(0)
    for copy in from_partner:
        copy.wait_recv()
    turn_near(1)

    def product(s, k, target):
        total = None
        for slot in range(4):
            value = jnp.dot(
                turned[s, target, :, block(slot, n_tok)], grads[s, k, block(slot, n_tok)],
                preferred_element_type=F32,
            ).astype(BF16).astype(F32)
            total = value if total is None else total + value
        return total

    def gathered(copies, last):
        copies[1].wait_recv()
        last.wait_recv()

    lasts, part_copies = {}, {}
    for s in range(2):
        lasts[s, 0] = forward(grads, s, 0, gathers[s, 0])
    for s in range(2):
        turn_side(s, False)
    for k in range(parts):
        for s in range(2):
            if k + 1 < parts:
                lasts[s, k + 1] = forward(grads, s, k + 1, gathers[s, k + 1])
            gathered(gathers[s, k], lasts[s, k])
            part_out[s, k] = product(s, k, 0).astype(BF16)
            part_copies[s, k] = send(part_out.at[s, k], part_in.at[s, k], {"dp": reduce_peer[s]})
    pass_on(True)
    for s in range(2):
        turn_side(s, True)
    moved_copies = {}
    for k in range(parts):
        for s in range(2):
            value = product(s, k, 1)
            part_copies[s, k].wait_recv()
            value = value + part_in[s, k].astype(F32)
            pert_ref[:, columns(s, k)] = value
            own, other = block(1 - s, rows), block(s, rows)
            moved[s, k, own] = value.astype(BF16)
            moved_copies[s, k] = send(
                moved.at[s, k, own], moved.at[s, k, other], {"dp": reduce_peer[s]}
            )

    squares = pert_ref[...]
    squares = squares * squares
    squares = jnp.sum(squares.reshape(rows // 8, 8, squares.shape[1]), axis=0)
    folded = squares[:, :128]
    for tile in range(1, squares.shape[1] // 128):
        folded = folded + squares[:, tile * 128:(tile + 1) * 128]
    total_dp[me] = folded
    dp_copies = [send(total_dp.at[me], total_dp.at[me], {"dp": peer}) for peer in dp_peers]

    def moving(s, tokens):
        if tokens < 2:
            return near[tokens, :, pl.ds(s * rows, 2 * rows)]
        return side[s, tokens - 2]

    def shift(s, k, tokens):
        return jnp.dot(moving(s, tokens), moved[s, k], preferred_element_type=F32)

    core_copies, side_copies = {}, {}

    def to_partner(s, k):
        moved_copies[s, k].wait_recv()
        core_out[s, k, 0] = shift(s, k, 3).astype(BF16)
        core_out[s, k, 1] = shift(s, k, 1).astype(BF16)
        core_copies[s, k] = send(core_out.at[s, k], core_in.at[s, k], {"dp": partner})

    def to_side(s, k):
        value = shift(s, k, 2)
        core_copies[s, k].wait_recv()
        side_out[s, k] = (value + core_in[s, k, 0].astype(F32)).astype(BF16)
        side_copies[s, k] = send(side_out.at[s, k], side_in.at[s, k], {"dp": gather_peer[s]})
        delta[s, k] = shift(s, k, 0) + core_in[s, k, 1].astype(F32)

    for s in range(2):
        to_partner(s, 0)
    for s in range(2):
        to_side(s, 0)
    for copy in dp_copies:
        copy.wait_recv()
    summed = total_dp[0]
    for shard in range(1, total_dp.shape[0]):
        summed = summed + total_dp[shard]
    total_mp[z] = summed
    mp_copies = [send(total_mp.at[z], total_mp.at[z], {"mp": peer}) for peer in mp_peers]
    for k in range(1, parts):
        for s in range(2):
            to_partner(s, k)
        for s in range(2):
            to_side(s, k)
    for copy in mp_copies:
        copy.wait_recv()
    summed = total_mp[0]
    for index in range(1, n_mp):
        summed = summed + total_mp[index]
    scale = radius / (jnp.sqrt(jnp.sum(summed, keepdims=True)) + 1e-12)

    for k in range(parts):
        for s in range(2):
            side_copies[s, k].wait_recv()
            query[:, columns(s, k)] += (delta[s, k] + side_in[s, k].astype(F32)) * scale
            gathers[s, k] = spread(grads2, s, k)
    pert_ref[...] = pert_ref[...] * scale

    sharp_copies = {}
    for s in range(2):
        lasts[s, 0] = forward(grads2, s, 0, gathers[s, 0])
    for k in range(parts):
        for s in range(2):
            if k + 1 < parts:
                lasts[s, k + 1] = forward(grads2, s, k + 1, gathers[s, k + 1])
            gathered(gathers[s, k], lasts[s, k])
            value = jnp.dot(turned[s, 0], grads2[s, k], preferred_element_type=F32)
            sharp_out[s, k] = value.astype(BF16)
            sharp_copies[s, k] = send(
                sharp_out.at[s, k], sharp_in.at[s, k], {"dp": reduce_peer[s]}
            )
    for k in range(parts):
        for s in range(2):
            sharp_ref[:, columns(s, k)] = jnp.dot(
                turned[s, 1], grads2[s, k], preferred_element_type=F32
            )
    for k in range(parts):
        for s in range(2):
            sharp_copies[s, k].wait_recv()
            sharp_ref[:, columns(s, k)] += sharp_in[s, k].astype(F32)
    for copy in started:
        copy.wait_send()


def cube_step(n_dp, n_mp, tokens, weight, norm_gain, upstream):
    n_tok, feat = tokens.shape
    columns = weight.shape[1]
    head_dim = norm_gain.shape[0]
    rows = feat // n_dp
    parts = columns // (2 * head_dim)
    radius = radius_coef * math.sqrt(feat * columns * n_mp)
    copies = 19 + 2 * parts * 11 + (n_dp - 1) + (n_mp - 1)
    vmem = pl.BlockSpec(memory_space=pltpu.VMEM)
    owned = pltpu.VMEM((rows, columns), F32)
    pieces = [
        pltpu.VMEM((2, parts, rows, head_dim), BF16),
        pltpu.VMEM((2, parts, rows, head_dim), BF16),
    ]
    return pl.pallas_call(
        functools.partial(cube_kernel, radius, n_mp),
        out_shape=(owned, owned),
        in_specs=[vmem, pl.BlockSpec(memory_space=pl.ANY), vmem, vmem],
        out_specs=(vmem, vmem),
        scratch_shapes=[
            pltpu.VMEM((feat, columns), BF16),
            pltpu.VMEM((n_tok, columns), F32),
            pltpu.VMEM((2, n_tok, 3 * rows), BF16),
            pltpu.VMEM((2, 2, n_tok, 2 * rows), BF16),
            pltpu.VMEM((2, 2, rows, 4 * n_tok), BF16),
            pltpu.VMEM((2, parts, 4 * n_tok, head_dim), BF16),
            pltpu.VMEM((2, parts, 4 * n_tok, head_dim), BF16),
        ]
        + pieces
        + [
            pltpu.VMEM((2, parts, 2 * rows, head_dim), BF16),
            pltpu.VMEM((2, parts, 2, n_tok, head_dim), BF16),
            pltpu.VMEM((2, parts, 2, n_tok, head_dim), BF16),
            pltpu.VMEM((2, parts, n_tok, head_dim), BF16),
            pltpu.VMEM((2, parts, n_tok, head_dim), BF16),
            pltpu.VMEM((2, parts, n_tok, head_dim), F32),
        ]
        + pieces
        + [
            pltpu.VMEM((n_dp, 8, 128), F32),
            pltpu.VMEM((n_mp, 8, 128), F32),
            pltpu.SemaphoreType.DMA((parts,)),
            pltpu.SemaphoreType.DMA((3,)),
            pltpu.SemaphoreType.DMA((copies,)),
            pltpu.SemaphoreType.DMA((copies,)),
        ],
        compiler_params=pltpu.CompilerParams(
            collective_id=0, has_side_effects=True, vmem_limit_bytes=60 * 1024 * 1024
        ),
        name="cube_step",
    )(tokens, weight, norm_gain.reshape(1, -1), upstream)


def solution(mesh):
    n_dp, n_mp = mesh.shape["dp"], mesh.shape["mp"]
    step = functools.partial(cube_step, n_dp, n_mp) if n_dp == 8 and n_mp % 2 == 0 else general_step
    in_specs = (P("dp", None), P(None, "mp"), P(), P("dp", "mp"))
    out_specs = (P("dp", "mp"), P("dp", "mp"))
    return jax.shard_map(
        step, mesh=mesh, in_specs=in_specs, out_specs=out_specs, check_vma=False
    )
```

```python
import functools
import math

import jax
import jax.numpy as jnp
from jax import lax
from jax.experimental import pallas as pl
from jax.experimental.pallas import tpu as pltpu
from jax.sharding import PartitionSpec as P

radius_coef = 0.004
RELAY = (96, 128)
EARLY = 0
F32 = jnp.float32
BF16 = jnp.bfloat16
MESH = pl.DeviceIdType.MESH


def head_backward(queries, upstream, norm_gain):
    head_dim = norm_gain.shape[0]
    count = queries.shape[0]
    grouped = queries.reshape(count, -1, head_dim)
    centred = grouped - jnp.mean(grouped, axis=-1, keepdims=True)
    inverse = lax.rsqrt(jnp.mean(centred * centred, axis=-1, keepdims=True) + 1e-06)
    normed = centred * inverse
    scaled = upstream.astype(jnp.float32).reshape(count, -1, head_dim) * norm_gain
    result = (
        scaled
        - jnp.mean(scaled, axis=-1, keepdims=True)
        - normed * jnp.mean(scaled * normed, axis=-1, keepdims=True)
    ) * inverse
    return result.reshape(count, -1).astype(jnp.bfloat16)


def left_product(left, right):
    return lax.dot_general(
        left, right, (((0,), (0,)), ((), ())), preferred_element_type=jnp.float32
    )


def general_step(tokens, weight, norm_gain, upstream):
    rows_own = weight.shape[0] // lax.axis_size("dp")
    radius = radius_coef * math.sqrt(weight.shape[0] * weight.shape[1] * lax.axis_size("mp"))
    row_start = lax.axis_index("dp") * rows_own
    first = jnp.dot(tokens, weight, preferred_element_type=jnp.float32)
    first_grad = head_backward(first, upstream, norm_gain)
    rounded = left_product(tokens, first_grad).astype(jnp.bfloat16)
    rounded = lax.optimization_barrier(rounded)
    owned = lax.psum_scatter(rounded.astype(jnp.float32), "dp", scatter_dimension=0, tiled=True)
    local_total = jnp.sum(owned * owned)
    total = lax.psum(local_total, ("dp", "mp"))
    perturbation = owned * (radius / (jnp.sqrt(total) + 1e-12))
    own_weight = lax.dynamic_slice_in_dim(weight, row_start, rows_own, 0)
    own_perturbed = (own_weight.astype(jnp.float32) + perturbation).astype(jnp.bfloat16)
    second = jnp.dot(
        tokens,
        lax.all_gather(own_perturbed, "dp", axis=0, tiled=True),
        preferred_element_type=jnp.float32,
    )
    second_grad = head_backward(second, upstream, norm_gain)
    sharp_grad = lax.psum_scatter(
        left_product(tokens, second_grad), "dp", scatter_dimension=0, tiled=True
    )
    return (perturbation, sharp_grad)


def cube_kernel(
    radius, n_mp,
    tok_hbm, w_hbm, gain_hbm, up_hbm,
    pert_ref, sharp_ref,
    tok_ref, gain_ref, up_ref, weight, query, near, side, turned, grads, grads2,
    part_out, part_in, moved, core_out, core_in, side_out, side_in, delta,
    sharp_out, sharp_in, total_dp, total_mp,
    load_sem, send_sem, recv_sem,
):
    n_tok = tok_ref.shape[0]
    rows = pert_ref.shape[0]
    parts, head_dim = grads.shape[1], grads.shape[3]
    me = lax.axis_index("dp")
    z = lax.axis_index("mp")
    y, x, c = me // 4, (me // 2) % 2, me % 2
    oy, ox, oc = 1 - y, 1 - x, 1 - c

    def at(yy, xx, cc):
        return (yy * 2 + xx) * 2 + cc

    partner, x_peer, y_peer = at(y, x, oc), at(y, ox, c), at(oy, x, c)
    x_cross, y_cross = at(y, ox, oc), at(oy, x, oc)
    diagonal, far = at(oy, ox, c), at(oy, ox, oc)
    dp_peers = [partner, x_peer, y_peer, x_cross, y_cross, diagonal, far]
    mp_peers = [lax.rem(z + k, n_mp) for k in range(1, n_mp)]
    parity = z % 2
    z_pair = z + 1 - 2 * parity

    barrier = pltpu.get_barrier_semaphore()
    for peer in dp_peers:
        pl.semaphore_signal(barrier, inc=1, device_id={"dp": peer}, device_id_type=MESH)
    for peer in mp_peers:
        pl.semaphore_signal(barrier, inc=1, device_id={"mp": peer}, device_id_type=MESH)

    gather_peer = [x_peer, y_peer]
    reduce_peer = [y_peer, x_peer]

    def columns(s, k):
        return pl.ds((2 * k + s) * head_dim, head_dim)

    def features(owner):
        return pl.ds(pl.multiple_of(owner * rows, rows), rows)

    def block(index, size):
        return pl.ds(index * size, size)

    loads = []

    def load(source, target):
        copy = pltpu.make_async_copy(source, target, load_sem.at[len(loads)])
        copy.start()
        loads.append(copy)
        return copy

    tok_load = load(tok_hbm, tok_ref)
    weight_loads = [
        load(w_hbm.at[:, block(k, 2 * head_dim)], weight.at[:, block(k, 2 * head_dim)])
        for k in range(parts)
    ]
    small_loads = [load(gain_hbm, gain_ref), load(up_hbm, up_ref)]
    near_copies = [
        load(tok_hbm.at[:, features(owner)], near.at[0, :, block(index, rows)])
        for index, owner in enumerate([y_peer, me, x_peer])
    ]

    started = []

    def send(source, target, device):
        index = len(started)
        copy = pltpu.make_async_remote_copy(
            src_ref=source, dst_ref=target,
            send_sem=send_sem.at[index], recv_sem=recv_sem.at[index],
            device_id=device, device_id_type=MESH,
        )
        copy.start()
        started.append(copy)
        return copy

    def relay(own):
        count = RELAY[own]
        return pl.ds(pl.multiple_of(parity * (n_tok - count), 16), count)

    def middle(own):
        return pl.ds(RELAY[own], n_tok - 2 * RELAY[own])

    brought = {}

    def bring(own, span, kind):
        for twin in range(2):
            cc = oc if twin else c
            for s in range(2):
                if s == 0:
                    receiver, owner = at(y, ox, cc), at(y if own else oy, ox, cc)
                else:
                    receiver, owner = at(oy, x, cc), at(oy, x if own else ox, cc)
                slot = 1 - s if own else s
                brought[s, own, twin, kind] = send(
                    tok_ref.at[span, features(owner)],
                    side.at[s, twin, span, block(slot, rows)], {"dp": receiver},
                )

    from_partner = []

    def bring_near():
        for index, owner in enumerate([at(oy, x, oc), partner, at(y, ox, oc)]):
            from_partner.append(
                send(tok_ref.at[:, features(owner)], near.at[1, :, block(index, rows)], {"dp": partner})
            )

    passed = {}

    def pass_on(own, twin):
        for s in range(2):
            brought[s, own, twin, 0].wait_recv()
            piece = side.at[s, twin, relay(own), block(1 - s if own else s, rows)]
            passed[s, own, twin] = send(piece, piece, {"mp": z_pair})

    def backward(out, s, k):
        half = n_tok // 2
        for low in (0, half):
            span = pl.ds(low, half)
            values = query[span, columns(s, k)]
            centred = values - jnp.mean(values, axis=-1, keepdims=True)
            inverse = lax.rsqrt(jnp.mean(centred * centred, axis=-1, keepdims=True) + 1e-06)
            normed = centred * inverse
            scaled = up_ref[span, columns(s, k)].astype(F32) * gain_ref[...]
            result = (
                scaled
                - jnp.mean(scaled, axis=-1, keepdims=True)
                - normed * jnp.mean(scaled * normed, axis=-1, keepdims=True)
            ) * inverse
            out[s, k, span] = result.astype(BF16)

    def spread(buffer, s, k):
        own = buffer.at[s, k, block(0, n_tok)]
        far_copy = send(own, buffer.at[s, k, block(2, n_tok)], {"dp": gather_peer[s]})
        near_copy = send(own, buffer.at[s, k, block(1, n_tok)], {"dp": partner})
        return far_copy, near_copy

    def forward(buffer, s, k, copies):
        copies[0].wait_recv()
        return send(
            buffer.at[s, k, block(2, n_tok)], buffer.at[s, k, block(3, n_tok)], {"dp": partner}
        )

    gathers = {}

    def first(k):
        weight_loads[k].wait()
        span = block(k, 2 * head_dim)
        query[:, span] = jnp.dot(tok_ref[...], weight[:, span], preferred_element_type=F32)
        if k == 0:
            for copy in small_loads:
                copy.wait()
        for s in range(2):
            backward(grads, s, k)

    tok_load.wait()
    for k in range(EARLY):
        first(k)
    pl.semaphore_wait(barrier, len(dp_peers) + len(mp_peers))
    for own in range(2):
        bring(own, relay(own), 0)
    for own in range(2):
        if 2 * RELAY[own] < n_tok:
            bring(own, middle(own), 1)
    for k in range(parts):
        if k >= EARLY:
            first(k)
        for s in range(2):
            gathers[s, k] = spread(grads, s, k)
        if k == 0:
            bring_near()

    for copy in near_copies:
        copy.wait()

    def turn_near(which):
        for index, places in enumerate([[(0, 0)], [(0, 1), (1, 1)], [(1, 0)]]):
            value = near[which, :, block(index, rows)].T
            for s, target in places:
                turned[s, target, :, block(which, n_tok)] = value

    def turn_side(s, own):
        for twin in range(2):
            if 2 * RELAY[own] < n_tok:
                brought[s, own, twin, 1].wait_recv()
            passed[s, own, twin].wait_recv()
            slot = 1 - s if own else s
            value = side[s, twin, :, block(slot, rows)].T
            turned[s, own, :, block(2 + twin, n_tok)] = value

    for twin in range(2):
        pass_on(0, twin)
    turn_near(0)
    for twin in range(2):
        pass_on(1, twin)
    for copy in from_partner:
        copy.wait_recv()
    turn_near(1)

    def product(s, k, target):
        total = None
        for slot in range(4):
            value = jnp.dot(
                turned[s, target, :, block(slot, n_tok)], grads[s, k, block(slot, n_tok)],
                preferred_element_type=F32,
            ).astype(BF16).astype(F32)
            total = value if total is None else total + value
        return total

    def gathered(copies, last):
        copies[1].wait_recv()
        last.wait_recv()

    lasts, part_copies = {}, {}
    for s in range(2):
        lasts[s, 0] = forward(grads, s, 0, gathers[s, 0])
    for s in range(2):
        turn_side(s, 0)
    for k in range(parts):
        for s in range(2):
            if k > 0:
                lasts[s, k] = forward(grads, s, k, gathers[s, k])
        for s in range(2):
            gathered(gathers[s, k], lasts[s, k])
            part_out[s, k] = product(s, k, 0).astype(BF16)
            part_copies[s, k] = send(part_out.at[s, k], part_in.at[s, k], {"dp": reduce_peer[s]})
    for s in range(2):
        turn_side(s, 1)
    moved_copies = {}

    def copy_moved(s, k):
        own, other = block(1 - s, rows), block(s, rows)
        moved_copies[s, k] = send(
            moved.at[s, k, own], moved.at[s, k, other], {"dp": reduce_peer[s]}
        )

    squares = None
    for k in range(parts):
        for s in range(2):
            value = product(s, k, 1)
            part_copies[s, k].wait_recv()
            value = value + part_in[s, k].astype(F32)
            pert_ref[:, columns(s, k)] = value
            moved[s, k, block(1 - s, rows)] = value.astype(BF16)
            square = jnp.sum((value * value).reshape(rows // 8, 8, head_dim), axis=0)
            squares = square if squares is None else squares + square
            if k + 1 < parts:
                copy_moved(s, k)
    total_dp[me] = squares
    dp_copies = [send(total_dp.at[me], total_dp.at[me], {"dp": peer}) for peer in dp_peers]
    for s in range(2):
        copy_moved(s, parts - 1)

    def moving(s, tokens):
        if tokens < 2:
            return near[tokens, :, pl.ds(s * rows, 2 * rows)]
        return side[s, tokens - 2]

    def shift(s, k, tokens):
        return jnp.dot(moving(s, tokens), moved[s, k], preferred_element_type=F32)

    core_copies, side_copies = {}, {}

    def to_partner(s, k):
        moved_copies[s, k].wait_recv()
        core_out[s, k, 0] = shift(s, k, 3).astype(BF16)
        core_out[s, k, 1] = shift(s, k, 1).astype(BF16)
        core_copies[s, k] = send(core_out.at[s, k], core_in.at[s, k], {"dp": partner})

    def to_side(s, k):
        value = shift(s, k, 2)
        core_copies[s, k].wait_recv()
        side_out[s, k] = (value + core_in[s, k, 0].astype(F32)).astype(BF16)
        side_copies[s, k] = send(side_out.at[s, k], side_in.at[s, k], {"dp": gather_peer[s]})
        delta[s, k] = shift(s, k, 0) + core_in[s, k, 1].astype(F32)

    for s in range(2):
        to_partner(s, 0)
    for s in range(2):
        to_side(s, 0)
    for copy in dp_copies:
        copy.wait_recv()
    summed = total_dp[0]
    for shard in range(1, total_dp.shape[0]):
        summed = summed + total_dp[shard]
    total_mp[z] = summed
    mp_copies = [send(total_mp.at[z], total_mp.at[z], {"mp": peer}) for peer in mp_peers]
    for k in range(1, parts):
        for s in range(2):
            to_partner(s, k)
        for s in range(2):
            to_side(s, k)
    for copy in mp_copies:
        copy.wait_recv()
    summed = total_mp[0]
    for index in range(1, n_mp):
        summed = summed + total_mp[index]
    scale = radius / (jnp.sqrt(jnp.sum(summed, keepdims=True)) + 1e-12)

    for k in range(parts):
        for s in range(2):
            side_copies[s, k].wait_recv()
            query[:, columns(s, k)] += (delta[s, k] + side_in[s, k].astype(F32)) * scale
            backward(grads2, s, k)
            gathers[s, k] = spread(grads2, s, k)
    pert_ref[...] = pert_ref[...] * scale

    sharp_copies = {}
    for s in range(2):
        lasts[s, 0] = forward(grads2, s, 0, gathers[s, 0])
    for k in range(parts):
        for s in range(2):
            if k + 1 < parts:
                lasts[s, k + 1] = forward(grads2, s, k + 1, gathers[s, k + 1])
            gathered(gathers[s, k], lasts[s, k])
            value = jnp.dot(turned[s, 0], grads2[s, k], preferred_element_type=F32)
            sharp_out[s, k] = value.astype(BF16)
            sharp_copies[s, k] = send(
                sharp_out.at[s, k], sharp_in.at[s, k], {"dp": reduce_peer[s]}
            )
    for k in range(parts):
        for s in range(2):
            sharp_ref[:, columns(s, k)] = jnp.dot(
                turned[s, 1], grads2[s, k], preferred_element_type=F32
            )
    for k in range(parts):
        for s in range(2):
            sharp_copies[s, k].wait_recv()
            sharp_ref[:, columns(s, k)] += sharp_in[s, k].astype(F32)
    for copy in started:
        copy.wait_send()


def cube_step(n_dp, n_mp, tokens, weight, norm_gain, upstream):
    n_tok, feat = tokens.shape
    columns = weight.shape[1]
    head_dim = norm_gain.shape[0]
    rows = feat // n_dp
    parts = columns // (2 * head_dim)
    radius = radius_coef * math.sqrt(feat * columns * n_mp)
    copies = 19 + 4 * sum(2 * count < n_tok for count in RELAY) + 2 * parts * 11 + (n_dp - 1) + (n_mp - 1)
    vmem = pl.BlockSpec(memory_space=pltpu.VMEM)
    owned = pltpu.VMEM((rows, columns), F32)
    pieces = [
        pltpu.VMEM((2, parts, rows, head_dim), BF16),
        pltpu.VMEM((2, parts, rows, head_dim), BF16),
    ]
    return pl.pallas_call(
        functools.partial(cube_kernel, radius, n_mp),
        out_shape=(owned, owned),
        in_specs=[pl.BlockSpec(memory_space=pl.ANY)] * 4,
        out_specs=(vmem, vmem),
        scratch_shapes=[
            pltpu.VMEM((n_tok, feat), BF16),
            pltpu.VMEM((1, head_dim), F32),
            pltpu.VMEM((n_tok, columns), BF16),
            pltpu.VMEM((feat, columns), BF16),
            pltpu.VMEM((n_tok, columns), F32),
            pltpu.VMEM((2, n_tok, 3 * rows), BF16),
            pltpu.VMEM((2, 2, n_tok, 2 * rows), BF16),
            pltpu.VMEM((2, 2, rows, 4 * n_tok), BF16),
            pltpu.VMEM((2, parts, 4 * n_tok, head_dim), BF16),
            pltpu.VMEM((2, parts, 4 * n_tok, head_dim), BF16),
        ]
        + pieces
        + [
            pltpu.VMEM((2, parts, 2 * rows, head_dim), BF16),
            pltpu.VMEM((2, parts, 2, n_tok, head_dim), BF16),
            pltpu.VMEM((2, parts, 2, n_tok, head_dim), BF16),
            pltpu.VMEM((2, parts, n_tok, head_dim), BF16),
            pltpu.VMEM((2, parts, n_tok, head_dim), BF16),
            pltpu.VMEM((2, parts, n_tok, head_dim), F32),
        ]
        + pieces
        + [
            pltpu.VMEM((n_dp, 8, 128), F32),
            pltpu.VMEM((n_mp, 8, 128), F32),
            pltpu.SemaphoreType.DMA((parts + 6,)),
            pltpu.SemaphoreType.DMA((copies,)),
            pltpu.SemaphoreType.DMA((copies,)),
        ],
        compiler_params=pltpu.CompilerParams(
            collective_id=0, has_side_effects=True, vmem_limit_bytes=60 * 1024 * 1024
        ),
        name="cube_step",
    )(tokens, weight, norm_gain.reshape(1, -1), upstream)


def solution(mesh):
    n_dp, n_mp = mesh.shape["dp"], mesh.shape["mp"]
    step = functools.partial(cube_step, n_dp, n_mp) if n_dp == 8 and n_mp % 2 == 0 else general_step
    in_specs = (P("dp", None), P(None, "mp"), P(), P("dp", "mp"))
    out_specs = (P("dp", "mp"), P("dp", "mp"))
    return jax.shard_map(
        step, mesh=mesh, in_specs=in_specs, out_specs=out_specs, check_vma=False
    )
```

```python
import functools
import math

import jax
import jax.numpy as jnp
from jax import lax
from jax.experimental import pallas as pl
from jax.experimental.pallas import tpu as pltpu
from jax.sharding import PartitionSpec as P

radius_coef = 0.004
RELAY = (96, 128)
EARLY = 0
F32 = jnp.float32
BF16 = jnp.bfloat16
MESH = pl.DeviceIdType.MESH


def head_backward(queries, upstream, norm_gain):
    head_dim = norm_gain.shape[0]
    count = queries.shape[0]
    grouped = queries.reshape(count, -1, head_dim)
    centred = grouped - jnp.mean(grouped, axis=-1, keepdims=True)
    inverse = lax.rsqrt(jnp.mean(centred * centred, axis=-1, keepdims=True) + 1e-06)
    normed = centred * inverse
    scaled = upstream.astype(jnp.float32).reshape(count, -1, head_dim) * norm_gain
    result = (
        scaled
        - jnp.mean(scaled, axis=-1, keepdims=True)
        - normed * jnp.mean(scaled * normed, axis=-1, keepdims=True)
    ) * inverse
    return result.reshape(count, -1).astype(jnp.bfloat16)


def left_product(left, right):
    return lax.dot_general(
        left, right, (((0,), (0,)), ((), ())), preferred_element_type=jnp.float32
    )


def general_step(tokens, weight, norm_gain, upstream):
    rows_own = weight.shape[0] // lax.axis_size("dp")
    radius = radius_coef * math.sqrt(weight.shape[0] * weight.shape[1] * lax.axis_size("mp"))
    row_start = lax.axis_index("dp") * rows_own
    first = jnp.dot(tokens, weight, preferred_element_type=jnp.float32)
    first_grad = head_backward(first, upstream, norm_gain)
    rounded = left_product(tokens, first_grad).astype(jnp.bfloat16)
    rounded = lax.optimization_barrier(rounded)
    owned = lax.psum_scatter(rounded.astype(jnp.float32), "dp", scatter_dimension=0, tiled=True)
    local_total = jnp.sum(owned * owned)
    total = lax.psum(local_total, ("dp", "mp"))
    perturbation = owned * (radius / (jnp.sqrt(total) + 1e-12))
    own_weight = lax.dynamic_slice_in_dim(weight, row_start, rows_own, 0)
    own_perturbed = (own_weight.astype(jnp.float32) + perturbation).astype(jnp.bfloat16)
    second = jnp.dot(
        tokens,
        lax.all_gather(own_perturbed, "dp", axis=0, tiled=True),
        preferred_element_type=jnp.float32,
    )
    second_grad = head_backward(second, upstream, norm_gain)
    sharp_grad = lax.psum_scatter(
        left_product(tokens, second_grad), "dp", scatter_dimension=0, tiled=True
    )
    return (perturbation, sharp_grad)


def cube_kernel(
    radius, n_mp,
    tok_hbm, w_hbm, gain_hbm, up_hbm,
    pert_ref, sharp_ref,
    tok_ref, gain_ref, up_ref, weight, query, near, side, turned, grads, grads2,
    part_out, part_in, moved, core_out, core_in, side_out, side_in, delta,
    sharp_out, sharp_in, total_dp, total_mp,
    load_sem, send_sem, recv_sem, hello,
):
    n_tok = tok_ref.shape[0]
    rows = pert_ref.shape[0]
    parts, head_dim = grads.shape[1], grads.shape[3]
    me = lax.axis_index("dp")
    z = lax.axis_index("mp")
    y, x, c = me // 4, (me // 2) % 2, me % 2
    oy, ox, oc = 1 - y, 1 - x, 1 - c

    def at(yy, xx, cc):
        return (yy * 2 + xx) * 2 + cc

    partner, x_peer, y_peer = at(y, x, oc), at(y, ox, c), at(oy, x, c)
    x_cross, y_cross = at(y, ox, oc), at(oy, x, oc)
    diagonal, far = at(oy, ox, c), at(oy, ox, oc)
    dp_peers = [partner, x_peer, y_peer, x_cross, y_cross, diagonal, far]
    mp_peers = [lax.rem(z + k, n_mp) for k in range(1, n_mp)]
    parity = z % 2
    z_pair = z + 1 - 2 * parity

    barrier = pltpu.get_barrier_semaphore()
    neighbours = [partner, x_peer, y_peer, x_cross, y_cross]
    for peer in neighbours:
        pl.semaphore_signal(barrier, inc=1, device_id={"dp": peer}, device_id_type=MESH)

    def signal_z(semaphore):
        @pl.when(z > 0)
        def _():
            pl.semaphore_signal(semaphore, inc=1, device_id={"mp": z - 1}, device_id_type=MESH)

        @pl.when(z < n_mp - 1)
        def _():
            pl.semaphore_signal(semaphore, inc=1, device_id={"mp": z + 1}, device_id_type=MESH)

    z_count = jnp.where(z > 0, 1, 0) + jnp.where(z < n_mp - 1, 1, 0)
    signal_z(barrier)

    gather_peer = [x_peer, y_peer]
    reduce_peer = [y_peer, x_peer]

    def columns(s, k):
        return pl.ds((2 * k + s) * head_dim, head_dim)

    def features(owner):
        return pl.ds(pl.multiple_of(owner * rows, rows), rows)

    def block(index, size):
        return pl.ds(index * size, size)

    loads = []

    def load(source, target):
        copy = pltpu.make_async_copy(source, target, load_sem.at[len(loads)])
        copy.start()
        loads.append(copy)
        return copy

    tok_load = load(tok_hbm, tok_ref)
    weight_loads = [
        load(w_hbm.at[:, block(k, 2 * head_dim)], weight.at[:, block(k, 2 * head_dim)])
        for k in range(parts)
    ]
    small_loads = [load(gain_hbm, gain_ref), load(up_hbm, up_ref)]
    near_copies = [
        load(tok_hbm.at[:, features(owner)], near.at[0, :, block(index, rows)])
        for index, owner in enumerate([y_peer, me, x_peer])
    ]

    started = []

    def send(source, target, device):
        index = len(started)
        copy = pltpu.make_async_remote_copy(
            src_ref=source, dst_ref=target,
            send_sem=send_sem.at[index], recv_sem=recv_sem.at[index],
            device_id=device, device_id_type=MESH,
        )
        copy.start()
        started.append(copy)
        return copy

    def relay(own):
        count = RELAY[own]
        return pl.ds(pl.multiple_of(parity * (n_tok - count), 16), count)

    def middle(own):
        return pl.ds(RELAY[own], n_tok - 2 * RELAY[own])

    brought = {}

    def bring(own, span, kind):
        for twin in range(2):
            cc = oc if twin else c
            for s in range(2):
                if s == 0:
                    receiver, owner = at(y, ox, cc), at(y if own else oy, ox, cc)
                else:
                    receiver, owner = at(oy, x, cc), at(oy, x if own else ox, cc)
                slot = 1 - s if own else s
                brought[s, own, twin, kind] = send(
                    tok_ref.at[span, features(owner)],
                    side.at[s, twin, span, block(slot, rows)], {"dp": receiver},
                )

    from_partner = []

    def bring_near():
        for index, owner in enumerate([at(oy, x, oc), partner, at(y, ox, oc)]):
            from_partner.append(
                send(tok_ref.at[:, features(owner)], near.at[1, :, block(index, rows)], {"dp": partner})
            )

    passed = {}

    def pass_on(own, twin):
        for s in range(2):
            brought[s, own, twin, 0].wait_recv()
            piece = side.at[s, twin, relay(own), block(1 - s if own else s, rows)]
            passed[s, own, twin] = send(piece, piece, {"mp": z_pair})

    def backward(out, s, k):
        half = n_tok // 2
        for low in (0, half):
            span = pl.ds(low, half)
            values = query[span, columns(s, k)]
            centred = values - jnp.mean(values, axis=-1, keepdims=True)
            inverse = lax.rsqrt(jnp.mean(centred * centred, axis=-1, keepdims=True) + 1e-06)
            normed = centred * inverse
            scaled = up_ref[span, columns(s, k)].astype(F32) * gain_ref[...]
            result = (
                scaled
                - jnp.mean(scaled, axis=-1, keepdims=True)
                - normed * jnp.mean(scaled * normed, axis=-1, keepdims=True)
            ) * inverse
            out[s, k, span] = result.astype(BF16)

    def spread(buffer, s, k):
        own = buffer.at[s, k, block(0, n_tok)]
        far_copy = send(own, buffer.at[s, k, block(2, n_tok)], {"dp": gather_peer[s]})
        near_copy = send(own, buffer.at[s, k, block(1, n_tok)], {"dp": partner})
        return far_copy, near_copy

    def forward(buffer, s, k, copies):
        copies[0].wait_recv()
        return send(
            buffer.at[s, k, block(2, n_tok)], buffer.at[s, k, block(3, n_tok)], {"dp": partner}
        )

    gathers = {}

    def first(k):
        weight_loads[k].wait()
        span = block(k, 2 * head_dim)
        query[:, span] = jnp.dot(tok_ref[...], weight[:, span], preferred_element_type=F32)
        if k == 0:
            for copy in small_loads:
                copy.wait()
        for s in range(2):
            backward(grads, s, k)

    tok_load.wait()
    for k in range(EARLY):
        first(k)
    pl.semaphore_wait(barrier, len(neighbours) + z_count)
    pl.semaphore_signal(hello.at[0], inc=1, device_id={"dp": y_peer}, device_id_type=MESH)
    signal_z(hello.at[1])
    for own in range(2):
        bring(own, relay(own), 0)
    for k in range(parts):
        if k >= EARLY:
            first(k)
        for s in range(2):
            gathers[s, k] = spread(grads, s, k)
        if k == 0:
            bring_near()
            for own in range(2):
                if 2 * RELAY[own] < n_tok:
                    bring(own, middle(own), 1)

    for copy in near_copies:
        copy.wait()

    def turn_near(which):
        for index, places in enumerate([[(0, 0)], [(0, 1), (1, 1)], [(1, 0)]]):
            value = near[which, :, block(index, rows)].T
            for s, target in places:
                turned[s, target, :, block(which, n_tok)] = value

    def turn_side(s, own):
        for twin in range(2):
            if 2 * RELAY[own] < n_tok:
                brought[s, own, twin, 1].wait_recv()
            passed[s, own, twin].wait_recv()
            slot = 1 - s if own else s
            value = side[s, twin, :, block(slot, rows)].T
            turned[s, own, :, block(2 + twin, n_tok)] = value

    for twin in range(2):
        pass_on(0, twin)
    for hop in range(1, n_mp - 2):
        pl.semaphore_wait(hello.at[hop], z_count)
        signal_z(hello.at[hop + 1])
    turn_near(0)
    for twin in range(2):
        pass_on(1, twin)
    for copy in from_partner:
        copy.wait_recv()
    turn_near(1)

    def product(s, k, target):
        total = None
        for slot in range(4):
            value = jnp.dot(
                turned[s, target, :, block(slot, n_tok)], grads[s, k, block(slot, n_tok)],
                preferred_element_type=F32,
            ).astype(BF16).astype(F32)
            total = value if total is None else total + value
        return total

    def gathered(copies, last):
        copies[1].wait_recv()
        last.wait_recv()

    lasts, part_copies = {}, {}
    for s in range(2):
        lasts[s, 0] = forward(grads, s, 0, gathers[s, 0])
    for s in range(2):
        turn_side(s, 0)
    for k in range(parts):
        for s in range(2):
            if k > 0:
                lasts[s, k] = forward(grads, s, k, gathers[s, k])
        for s in range(2):
            gathered(gathers[s, k], lasts[s, k])
            part_out[s, k] = product(s, k, 0).astype(BF16)
            part_copies[s, k] = send(part_out.at[s, k], part_in.at[s, k], {"dp": reduce_peer[s]})
    for s in range(2):
        turn_side(s, 1)
    moved_copies = {}

    def copy_moved(s, k):
        own, other = block(1 - s, rows), block(s, rows)
        moved_copies[s, k] = send(
            moved.at[s, k, own], moved.at[s, k, other], {"dp": reduce_peer[s]}
        )

    squares = None
    for k in range(parts):
        for s in range(2):
            value = product(s, k, 1)
            part_copies[s, k].wait_recv()
            value = value + part_in[s, k].astype(F32)
            pert_ref[:, columns(s, k)] = value
            moved[s, k, block(1 - s, rows)] = value.astype(BF16)
            square = jnp.sum((value * value).reshape(rows // 8, 8, head_dim), axis=0)
            squares = square if squares is None else squares + square
            if k + 1 < parts:
                copy_moved(s, k)
    pl.semaphore_wait(hello.at[0], 1)
    pl.semaphore_wait(hello.at[n_mp - 2], z_count)
    total_dp[me] = squares
    dp_copies = [send(total_dp.at[me], total_dp.at[me], {"dp": peer}) for peer in dp_peers]
    for s in range(2):
        copy_moved(s, parts - 1)

    def moving(s, tokens):
        if tokens < 2:
            return near[tokens, :, pl.ds(s * rows, 2 * rows)]
        return side[s, tokens - 2]

    def shift(s, k, tokens):
        return jnp.dot(moving(s, tokens), moved[s, k], preferred_element_type=F32)

    def update(s, k):
        side_copies[s, k].wait_recv()
        query[:, columns(s, k)] += (delta[s, k] + side_in[s, k].astype(F32)) * scale
        backward(grads2, s, k)
        gathers[s, k] = spread(grads2, s, k)

    core_copies, side_copies = {}, {}

    def to_partner(s, k):
        moved_copies[s, k].wait_recv()
        core_out[s, k, 0] = shift(s, k, 3).astype(BF16)
        core_out[s, k, 1] = shift(s, k, 1).astype(BF16)
        core_copies[s, k] = send(core_out.at[s, k], core_in.at[s, k], {"dp": partner})

    def to_side(s, k):
        value = shift(s, k, 2)
        core_copies[s, k].wait_recv()
        side_out[s, k] = (value + core_in[s, k, 0].astype(F32)).astype(BF16)
        side_copies[s, k] = send(side_out.at[s, k], side_in.at[s, k], {"dp": gather_peer[s]})
        delta[s, k] = shift(s, k, 0) + core_in[s, k, 1].astype(F32)

    for s in range(2):
        to_partner(s, 0)
    for s in range(2):
        to_side(s, 0)
    for copy in dp_copies:
        copy.wait_recv()
    summed = total_dp[0]
    for shard in range(1, total_dp.shape[0]):
        summed = summed + total_dp[shard]
    total_mp[z] = summed
    mp_copies = [send(total_mp.at[z], total_mp.at[z], {"mp": peer}) for peer in mp_peers]
    for k in range(1, parts - 1):
        for s in range(2):
            to_partner(s, k)
        for s in range(2):
            to_side(s, k)
    for s in range(2):
        to_partner(s, parts - 1)
    for copy in mp_copies:
        copy.wait_recv()
    summed = total_mp[0]
    for index in range(1, n_mp):
        summed = summed + total_mp[index]
    scale = radius / (jnp.sqrt(jnp.sum(summed, keepdims=True)) + 1e-12)
    for s in range(2):
        update(s, 0)
    for s in range(2):
        to_side(s, parts - 1)
    for k in range(1, parts):
        for s in range(2):
            update(s, k)
    pert_ref[...] = pert_ref[...] * scale

    sharp_copies = {}
    for s in range(2):
        lasts[s, 0] = forward(grads2, s, 0, gathers[s, 0])
    for k in range(parts):
        for s in range(2):
            if k + 1 < parts:
                lasts[s, k + 1] = forward(grads2, s, k + 1, gathers[s, k + 1])
            gathered(gathers[s, k], lasts[s, k])
            value = jnp.dot(turned[s, 0], grads2[s, k], preferred_element_type=F32)
            sharp_out[s, k] = value.astype(BF16)
            sharp_copies[s, k] = send(
                sharp_out.at[s, k], sharp_in.at[s, k], {"dp": reduce_peer[s]}
            )
    for k in range(parts):
        for s in range(2):
            sharp_ref[:, columns(s, k)] = jnp.dot(
                turned[s, 1], grads2[s, k], preferred_element_type=F32
            )
    for k in range(parts):
        for s in range(2):
            sharp_copies[s, k].wait_recv()
            sharp_ref[:, columns(s, k)] += sharp_in[s, k].astype(F32)
    for copy in started:
        copy.wait_send()


def cube_step(n_dp, n_mp, tokens, weight, norm_gain, upstream):
    n_tok, feat = tokens.shape
    columns = weight.shape[1]
    head_dim = norm_gain.shape[0]
    rows = feat // n_dp
    parts = columns // (2 * head_dim)
    radius = radius_coef * math.sqrt(feat * columns * n_mp)
    copies = 19 + 4 * sum(2 * count < n_tok for count in RELAY) + 2 * parts * 11 + (n_dp - 1) + (n_mp - 1)
    vmem = pl.BlockSpec(memory_space=pltpu.VMEM)
    owned = pltpu.VMEM((rows, columns), F32)
    pieces = [
        pltpu.VMEM((2, parts, rows, head_dim), BF16),
        pltpu.VMEM((2, parts, rows, head_dim), BF16),
    ]
    return pl.pallas_call(
        functools.partial(cube_kernel, radius, n_mp),
        out_shape=(owned, owned),
        in_specs=[pl.BlockSpec(memory_space=pl.ANY)] * 4,
        out_specs=(vmem, vmem),
        scratch_shapes=[
            pltpu.VMEM((n_tok, feat), BF16),
            pltpu.VMEM((1, head_dim), F32),
            pltpu.VMEM((n_tok, columns), BF16),
            pltpu.VMEM((feat, columns), BF16),
            pltpu.VMEM((n_tok, columns), F32),
            pltpu.VMEM((2, n_tok, 3 * rows), BF16),
            pltpu.VMEM((2, 2, n_tok, 2 * rows), BF16),
            pltpu.VMEM((2, 2, rows, 4 * n_tok), BF16),
            pltpu.VMEM((2, parts, 4 * n_tok, head_dim), BF16),
            pltpu.VMEM((2, parts, 4 * n_tok, head_dim), BF16),
        ]
        + pieces
        + [
            pltpu.VMEM((2, parts, 2 * rows, head_dim), BF16),
            pltpu.VMEM((2, parts, 2, n_tok, head_dim), BF16),
            pltpu.VMEM((2, parts, 2, n_tok, head_dim), BF16),
            pltpu.VMEM((2, parts, n_tok, head_dim), BF16),
            pltpu.VMEM((2, parts, n_tok, head_dim), BF16),
            pltpu.VMEM((2, parts, n_tok, head_dim), F32),
        ]
        + pieces
        + [
            pltpu.VMEM((n_dp, 8, 128), F32),
            pltpu.VMEM((n_mp, 8, 128), F32),
            pltpu.SemaphoreType.DMA((parts + 6,)),
            pltpu.SemaphoreType.DMA((copies,)),
            pltpu.SemaphoreType.DMA((copies,)),
            pltpu.SemaphoreType.REGULAR((n_mp - 1,)),
        ],
        compiler_params=pltpu.CompilerParams(
            collective_id=0, has_side_effects=True, vmem_limit_bytes=60 * 1024 * 1024
        ),
        name="cube_step",
    )(tokens, weight, norm_gain.reshape(1, -1), upstream)


def solution(mesh):
    n_dp, n_mp = mesh.shape["dp"], mesh.shape["mp"]
    step = functools.partial(cube_step, n_dp, n_mp) if n_dp == 8 and n_mp == 4 else general_step
    in_specs = (P("dp", None), P(None, "mp"), P(), P("dp", "mp"))
    out_specs = (P("dp", "mp"), P("dp", "mp"))
    return jax.shard_map(
        step, mesh=mesh, in_specs=in_specs, out_specs=out_specs, check_vma=False
    )
```

```python
import functools
import math

import jax
import jax.numpy as jnp
from jax import lax
from jax.experimental import pallas as pl
from jax.experimental.pallas import tpu as pltpu
from jax.sharding import PartitionSpec as P

radius_coef = 0.004
RELAY = (96, 112)
EARLY = 0
F32 = jnp.float32
BF16 = jnp.bfloat16
MESH = pl.DeviceIdType.MESH


def head_backward(queries, upstream, norm_gain):
    head_dim = norm_gain.shape[0]
    count = queries.shape[0]
    grouped = queries.reshape(count, -1, head_dim)
    centred = grouped - jnp.mean(grouped, axis=-1, keepdims=True)
    inverse = lax.rsqrt(jnp.mean(centred * centred, axis=-1, keepdims=True) + 1e-06)
    normed = centred * inverse
    scaled = upstream.astype(jnp.float32).reshape(count, -1, head_dim) * norm_gain
    result = (
        scaled
        - jnp.mean(scaled, axis=-1, keepdims=True)
        - normed * jnp.mean(scaled * normed, axis=-1, keepdims=True)
    ) * inverse
    return result.reshape(count, -1).astype(jnp.bfloat16)


def left_product(left, right):
    return lax.dot_general(
        left, right, (((0,), (0,)), ((), ())), preferred_element_type=jnp.float32
    )


def general_step(tokens, weight, norm_gain, upstream):
    rows_own = weight.shape[0] // lax.axis_size("dp")
    radius = radius_coef * math.sqrt(weight.shape[0] * weight.shape[1] * lax.axis_size("mp"))
    row_start = lax.axis_index("dp") * rows_own
    first = jnp.dot(tokens, weight, preferred_element_type=jnp.float32)
    first_grad = head_backward(first, upstream, norm_gain)
    rounded = left_product(tokens, first_grad).astype(jnp.bfloat16)
    rounded = lax.optimization_barrier(rounded)
    owned = lax.psum_scatter(rounded.astype(jnp.float32), "dp", scatter_dimension=0, tiled=True)
    local_total = jnp.sum(owned * owned)
    total = lax.psum(local_total, ("dp", "mp"))
    perturbation = owned * (radius / (jnp.sqrt(total) + 1e-12))
    own_weight = lax.dynamic_slice_in_dim(weight, row_start, rows_own, 0)
    own_perturbed = (own_weight.astype(jnp.float32) + perturbation).astype(jnp.bfloat16)
    second = jnp.dot(
        tokens,
        lax.all_gather(own_perturbed, "dp", axis=0, tiled=True),
        preferred_element_type=jnp.float32,
    )
    second_grad = head_backward(second, upstream, norm_gain)
    sharp_grad = lax.psum_scatter(
        left_product(tokens, second_grad), "dp", scatter_dimension=0, tiled=True
    )
    return (perturbation, sharp_grad)


def cube_kernel(
    radius, n_mp,
    tok_hbm, w_hbm, gain_hbm, up_hbm,
    pert_ref, sharp_ref,
    tok_ref, gain_ref, up_ref, weight, query, near, side, turned, grads, grads2,
    part_out, part_in, moved, core_out, core_in, side_out, side_in, delta,
    sharp_out, sharp_in, total_dp, total_mp,
    load_sem, send_sem, recv_sem, hello,
):
    n_tok = tok_ref.shape[0]
    rows = pert_ref.shape[0]
    parts, head_dim = grads.shape[1], grads.shape[3]
    me = lax.axis_index("dp")
    z = lax.axis_index("mp")
    y, x, c = me // 4, (me // 2) % 2, me % 2
    oy, ox, oc = 1 - y, 1 - x, 1 - c

    def at(yy, xx, cc):
        return (yy * 2 + xx) * 2 + cc

    partner, x_peer, y_peer = at(y, x, oc), at(y, ox, c), at(oy, x, c)
    x_cross, y_cross = at(y, ox, oc), at(oy, x, oc)
    diagonal, far = at(oy, ox, c), at(oy, ox, oc)
    dp_peers = [partner, x_peer, y_peer, x_cross, y_cross, diagonal, far]
    mp_peers = [lax.rem(z + k, n_mp) for k in range(1, n_mp)]
    parity = z % 2
    z_pair = z + 1 - 2 * parity

    barrier = pltpu.get_barrier_semaphore()
    neighbours = [partner, x_peer, y_peer, x_cross, y_cross]
    for peer in neighbours:
        pl.semaphore_signal(barrier, inc=1, device_id={"dp": peer}, device_id_type=MESH)

    def signal_z(semaphore):
        @pl.when(z > 0)
        def _():
            pl.semaphore_signal(semaphore, inc=1, device_id={"mp": z - 1}, device_id_type=MESH)

        @pl.when(z < n_mp - 1)
        def _():
            pl.semaphore_signal(semaphore, inc=1, device_id={"mp": z + 1}, device_id_type=MESH)

    z_count = jnp.where(z > 0, 1, 0) + jnp.where(z < n_mp - 1, 1, 0)
    signal_z(barrier)

    gather_peer = [x_peer, y_peer]
    reduce_peer = [y_peer, x_peer]

    def columns(s, k):
        return pl.ds((2 * k + s) * head_dim, head_dim)

    def features(owner):
        return pl.ds(pl.multiple_of(owner * rows, rows), rows)

    def block(index, size):
        return pl.ds(index * size, size)

    loads = []

    def load(source, target):
        copy = pltpu.make_async_copy(source, target, load_sem.at[len(loads)])
        copy.start()
        loads.append(copy)
        return copy

    tok_load = load(tok_hbm, tok_ref)
    weight_loads = [
        load(w_hbm.at[:, block(k, 2 * head_dim)], weight.at[:, block(k, 2 * head_dim)])
        for k in range(parts)
    ]
    small_loads = [load(gain_hbm, gain_ref), load(up_hbm, up_ref)]
    near_copies = [
        load(tok_hbm.at[:, features(owner)], near.at[0, :, block(index, rows)])
        for index, owner in enumerate([y_peer, me, x_peer])
    ]

    started = []

    def send(source, target, device):
        index = len(started)
        copy = pltpu.make_async_remote_copy(
            src_ref=source, dst_ref=target,
            send_sem=send_sem.at[index], recv_sem=recv_sem.at[index],
            device_id=device, device_id_type=MESH,
        )
        copy.start()
        started.append(copy)
        return copy

    def relay(own):
        count = RELAY[own]
        return pl.ds(pl.multiple_of(parity * (n_tok - count), 16), count)

    def middle(own):
        return pl.ds(RELAY[own], n_tok - 2 * RELAY[own])

    brought = {}

    def bring(own, span, kind):
        for twin in range(2):
            cc = oc if twin else c
            for s in range(2):
                if s == 0:
                    receiver, owner = at(y, ox, cc), at(y if own else oy, ox, cc)
                else:
                    receiver, owner = at(oy, x, cc), at(oy, x if own else ox, cc)
                slot = 1 - s if own else s
                brought[s, own, twin, kind] = send(
                    tok_ref.at[span, features(owner)],
                    side.at[s, twin, span, block(slot, rows)], {"dp": receiver},
                )

    from_partner = []

    def bring_near():
        for index, owner in enumerate([at(oy, x, oc), partner, at(y, ox, oc)]):
            from_partner.append(
                send(tok_ref.at[:, features(owner)], near.at[1, :, block(index, rows)], {"dp": partner})
            )

    passed = {}

    def pass_on(own, twin):
        for s in range(2):
            brought[s, own, twin, 0].wait_recv()
            piece = side.at[s, twin, relay(own), block(1 - s if own else s, rows)]
            passed[s, own, twin] = send(piece, piece, {"mp": z_pair})

    def backward(out, s, k):
        half = n_tok // 2
        for low in (0, half):
            span = pl.ds(low, half)
            values = query[span, columns(s, k)]
            centred = values - jnp.mean(values, axis=-1, keepdims=True)
            inverse = lax.rsqrt(jnp.mean(centred * centred, axis=-1, keepdims=True) + 1e-06)
            normed = centred * inverse
            scaled = up_ref[span, columns(s, k)].astype(F32) * gain_ref[...]
            result = (
                scaled
                - jnp.mean(scaled, axis=-1, keepdims=True)
                - normed * jnp.mean(scaled * normed, axis=-1, keepdims=True)
            ) * inverse
            out[s, k, span] = result.astype(BF16)

    def spread(buffer, s, k):
        own = buffer.at[s, k, block(0, n_tok)]
        far_copy = send(own, buffer.at[s, k, block(2, n_tok)], {"dp": gather_peer[s]})
        near_copy = send(own, buffer.at[s, k, block(1, n_tok)], {"dp": partner})
        return far_copy, near_copy

    def forward(buffer, s, k, copies):
        copies[0].wait_recv()
        return send(
            buffer.at[s, k, block(2, n_tok)], buffer.at[s, k, block(3, n_tok)], {"dp": partner}
        )

    gathers = {}

    def first(k):
        weight_loads[k].wait()
        span = block(k, 2 * head_dim)
        query[:, span] = jnp.dot(tok_ref[...], weight[:, span], preferred_element_type=F32)
        if k == 0:
            for copy in small_loads:
                copy.wait()
        for s in range(2):
            backward(grads, s, k)

    tok_load.wait()
    for k in range(EARLY):
        first(k)
    pl.semaphore_wait(barrier, len(neighbours) + z_count)
    pl.semaphore_signal(hello.at[0], inc=1, device_id={"dp": y_peer}, device_id_type=MESH)
    signal_z(hello.at[1])
    for own in range(2):
        bring(own, relay(own), 0)
    for k in range(parts):
        if k >= EARLY:
            first(k)
        for s in range(2):
            gathers[s, k] = spread(grads, s, k)
        if k == 0:
            bring_near()
            for own in range(2):
                if 2 * RELAY[own] < n_tok:
                    bring(own, middle(own), 1)

    for copy in near_copies:
        copy.wait()

    def turn_near(which):
        for index, places in enumerate([[(0, 0)], [(0, 1), (1, 1)], [(1, 0)]]):
            value = near[which, :, block(index, rows)].T
            for s, target in places:
                turned[s, target, :, block(which, n_tok)] = value

    def turn_side(s, own):
        for twin in range(2):
            if 2 * RELAY[own] < n_tok:
                brought[s, own, twin, 1].wait_recv()
            passed[s, own, twin].wait_recv()
            slot = 1 - s if own else s
            value = side[s, twin, :, block(slot, rows)].T
            turned[s, own, :, block(2 + twin, n_tok)] = value

    for twin in range(2):
        pass_on(0, twin)
    for hop in range(1, n_mp - 2):
        pl.semaphore_wait(hello.at[hop], z_count)
        signal_z(hello.at[hop + 1])
    turn_near(0)
    for twin in range(2):
        pass_on(1, twin)
    for copy in from_partner:
        copy.wait_recv()
    turn_near(1)

    def product(s, k, target):
        total = None
        for slot in range(4):
            value = jnp.dot(
                turned[s, target, :, block(slot, n_tok)], grads[s, k, block(slot, n_tok)],
                preferred_element_type=F32,
            ).astype(BF16).astype(F32)
            total = value if total is None else total + value
        return total

    def gathered(copies, last):
        copies[1].wait_recv()
        last.wait_recv()

    lasts, part_copies = {}, {}
    for s in range(2):
        lasts[s, 0] = forward(grads, s, 0, gathers[s, 0])
    for s in range(2):
        turn_side(s, 0)
    for k in range(parts):
        for s in range(2):
            if k > 0:
                lasts[s, k] = forward(grads, s, k, gathers[s, k])
        for s in range(2):
            gathered(gathers[s, k], lasts[s, k])
            part_out[s, k] = product(s, k, 0).astype(BF16)
            part_copies[s, k] = send(part_out.at[s, k], part_in.at[s, k], {"dp": reduce_peer[s]})
    for s in range(2):
        turn_side(s, 1)
    moved_copies = {}

    def copy_moved(s, k):
        own, other = block(1 - s, rows), block(s, rows)
        moved_copies[s, k] = send(
            moved.at[s, k, own], moved.at[s, k, other], {"dp": reduce_peer[s]}
        )

    squares = None
    for k in range(parts):
        for s in range(2):
            value = product(s, k, 1)
            part_copies[s, k].wait_recv()
            value = value + part_in[s, k].astype(F32)
            pert_ref[:, columns(s, k)] = value
            moved[s, k, block(1 - s, rows)] = value.astype(BF16)
            square = jnp.sum((value * value).reshape(rows // 8, 8, head_dim), axis=0)
            squares = square if squares is None else squares + square
            if k + 2 < parts:
                copy_moved(s, k)
    pl.semaphore_wait(hello.at[0], 1)
    pl.semaphore_wait(hello.at[n_mp - 2], z_count)
    total_dp[me] = squares
    dp_copies = [send(total_dp.at[me], total_dp.at[me], {"dp": peer}) for peer in dp_peers]
    for k in range(parts - 2, parts):
        for s in range(2):
            copy_moved(s, k)

    def moving(s, tokens):
        if tokens < 2:
            return near[tokens, :, pl.ds(s * rows, 2 * rows)]
        return side[s, tokens - 2]

    def shift(s, k, tokens):
        return jnp.dot(moving(s, tokens), moved[s, k], preferred_element_type=F32)

    def update(s, k):
        side_copies[s, k].wait_recv()
        query[:, columns(s, k)] += (delta[s, k] + side_in[s, k].astype(F32)) * scale
        backward(grads2, s, k)
        gathers[s, k] = spread(grads2, s, k)

    core_copies, side_copies = {}, {}

    def to_partner(s, k):
        moved_copies[s, k].wait_recv()
        core_out[s, k, 0] = shift(s, k, 3).astype(BF16)
        core_out[s, k, 1] = shift(s, k, 1).astype(BF16)
        core_copies[s, k] = send(core_out.at[s, k], core_in.at[s, k], {"dp": partner})

    def to_side(s, k):
        value = shift(s, k, 2)
        core_copies[s, k].wait_recv()
        side_out[s, k] = (value + core_in[s, k, 0].astype(F32)).astype(BF16)
        side_copies[s, k] = send(side_out.at[s, k], side_in.at[s, k], {"dp": gather_peer[s]})
        delta[s, k] = shift(s, k, 0) + core_in[s, k, 1].astype(F32)

    for s in range(2):
        to_partner(s, 0)
    for copy in dp_copies:
        copy.wait_recv()
    summed = total_dp[0]
    for shard in range(1, total_dp.shape[0]):
        summed = summed + total_dp[shard]
    total_mp[z] = summed
    mp_copies = [send(total_mp.at[z], total_mp.at[z], {"mp": peer}) for peer in mp_peers]
    for s in range(2):
        to_side(s, 0)
    for k in range(1, parts - 1):
        for s in range(2):
            to_partner(s, k)
        for s in range(2):
            to_side(s, k)
    for s in range(2):
        to_partner(s, parts - 1)
    for copy in mp_copies:
        copy.wait_recv()
    summed = total_mp[0]
    for index in range(1, n_mp):
        summed = summed + total_mp[index]
    scale = radius / (jnp.sqrt(jnp.sum(summed, keepdims=True)) + 1e-12)
    for s in range(2):
        update(s, 0)
    for s in range(2):
        to_side(s, parts - 1)
    for k in range(1, parts):
        for s in range(2):
            update(s, k)
    pert_ref[...] = pert_ref[...] * scale

    sharp_copies = {}
    for k in range(parts):
        for s in range(2):
            lasts[s, k] = forward(grads2, s, k, gathers[s, k])
        for s in range(2):
            gathered(gathers[s, k], lasts[s, k])
            value = jnp.dot(turned[s, 0], grads2[s, k], preferred_element_type=F32)
            sharp_out[s, k] = value.astype(BF16)
            sharp_copies[s, k] = send(
                sharp_out.at[s, k], sharp_in.at[s, k], {"dp": reduce_peer[s]}
            )
    for k in range(parts):
        for s in range(2):
            sharp_ref[:, columns(s, k)] = jnp.dot(
                turned[s, 1], grads2[s, k], preferred_element_type=F32
            )
    for k in range(parts):
        for s in range(2):
            sharp_copies[s, k].wait_recv()
            sharp_ref[:, columns(s, k)] += sharp_in[s, k].astype(F32)
    for copy in started:
        copy.wait_send()


def cube_step(n_dp, n_mp, tokens, weight, norm_gain, upstream):
    n_tok, feat = tokens.shape
    columns = weight.shape[1]
    head_dim = norm_gain.shape[0]
    rows = feat // n_dp
    parts = columns // (2 * head_dim)
    radius = radius_coef * math.sqrt(feat * columns * n_mp)
    copies = 19 + 4 * sum(2 * count < n_tok for count in RELAY) + 2 * parts * 11 + (n_dp - 1) + (n_mp - 1)
    vmem = pl.BlockSpec(memory_space=pltpu.VMEM)
    owned = pltpu.VMEM((rows, columns), F32)
    pieces = [
        pltpu.VMEM((2, parts, rows, head_dim), BF16),
        pltpu.VMEM((2, parts, rows, head_dim), BF16),
    ]
    return pl.pallas_call(
        functools.partial(cube_kernel, radius, n_mp),
        out_shape=(owned, owned),
        in_specs=[pl.BlockSpec(memory_space=pl.ANY)] * 4,
        out_specs=(vmem, vmem),
        scratch_shapes=[
            pltpu.VMEM((n_tok, feat), BF16),
            pltpu.VMEM((1, head_dim), F32),
            pltpu.VMEM((n_tok, columns), BF16),
            pltpu.VMEM((feat, columns), BF16),
            pltpu.VMEM((n_tok, columns), F32),
            pltpu.VMEM((2, n_tok, 3 * rows), BF16),
            pltpu.VMEM((2, 2, n_tok, 2 * rows), BF16),
            pltpu.VMEM((2, 2, rows, 4 * n_tok), BF16),
            pltpu.VMEM((2, parts, 4 * n_tok, head_dim), BF16),
            pltpu.VMEM((2, parts, 4 * n_tok, head_dim), BF16),
        ]
        + pieces
        + [
            pltpu.VMEM((2, parts, 2 * rows, head_dim), BF16),
            pltpu.VMEM((2, parts, 2, n_tok, head_dim), BF16),
            pltpu.VMEM((2, parts, 2, n_tok, head_dim), BF16),
            pltpu.VMEM((2, parts, n_tok, head_dim), BF16),
            pltpu.VMEM((2, parts, n_tok, head_dim), BF16),
            pltpu.VMEM((2, parts, n_tok, head_dim), F32),
        ]
        + pieces
        + [
            pltpu.VMEM((n_dp, 8, 128), F32),
            pltpu.VMEM((n_mp, 8, 128), F32),
            pltpu.SemaphoreType.DMA((parts + 6,)),
            pltpu.SemaphoreType.DMA((copies,)),
            pltpu.SemaphoreType.DMA((copies,)),
            pltpu.SemaphoreType.REGULAR((n_mp - 1,)),
        ],
        compiler_params=pltpu.CompilerParams(
            collective_id=0, has_side_effects=True, vmem_limit_bytes=60 * 1024 * 1024
        ),
        name="cube_step",
    )(tokens, weight, norm_gain.reshape(1, -1), upstream)


def solution(mesh):
    n_dp, n_mp = mesh.shape["dp"], mesh.shape["mp"]
    step = functools.partial(cube_step, n_dp, n_mp) if n_dp == 8 and n_mp == 4 else general_step
    in_specs = (P("dp", None), P(None, "mp"), P(), P("dp", "mp"))
    out_specs = (P("dp", "mp"), P("dp", "mp"))
    return jax.shard_map(
        step, mesh=mesh, in_specs=in_specs, out_specs=out_specs, check_vma=False
    )
```

```python
import functools
import math

import jax
import jax.numpy as jnp
from jax import lax
from jax.experimental import pallas as pl
from jax.experimental.pallas import tpu as pltpu
from jax.sharding import PartitionSpec as P

radius_coef = 0.004
RELAY = (96, 128)
EARLY = 0
F32 = jnp.float32
BF16 = jnp.bfloat16
MESH = pl.DeviceIdType.MESH


def head_backward(queries, upstream, norm_gain):
    head_dim = norm_gain.shape[0]
    count = queries.shape[0]
    grouped = queries.reshape(count, -1, head_dim)
    centred = grouped - jnp.mean(grouped, axis=-1, keepdims=True)
    inverse = lax.rsqrt(jnp.mean(centred * centred, axis=-1, keepdims=True) + 1e-06)
    normed = centred * inverse
    scaled = upstream.astype(jnp.float32).reshape(count, -1, head_dim) * norm_gain
    result = (
        scaled
        - jnp.mean(scaled, axis=-1, keepdims=True)
        - normed * jnp.mean(scaled * normed, axis=-1, keepdims=True)
    ) * inverse
    return result.reshape(count, -1).astype(jnp.bfloat16)


def left_product(left, right):
    return lax.dot_general(
        left, right, (((0,), (0,)), ((), ())), preferred_element_type=jnp.float32
    )


def general_step(tokens, weight, norm_gain, upstream):
    rows_own = weight.shape[0] // lax.axis_size("dp")
    radius = radius_coef * math.sqrt(weight.shape[0] * weight.shape[1] * lax.axis_size("mp"))
    row_start = lax.axis_index("dp") * rows_own
    first = jnp.dot(tokens, weight, preferred_element_type=jnp.float32)
    first_grad = head_backward(first, upstream, norm_gain)
    rounded = left_product(tokens, first_grad).astype(jnp.bfloat16)
    rounded = lax.optimization_barrier(rounded)
    owned = lax.psum_scatter(rounded.astype(jnp.float32), "dp", scatter_dimension=0, tiled=True)
    local_total = jnp.sum(owned * owned)
    total = lax.psum(local_total, ("dp", "mp"))
    perturbation = owned * (radius / (jnp.sqrt(total) + 1e-12))
    own_weight = lax.dynamic_slice_in_dim(weight, row_start, rows_own, 0)
    own_perturbed = (own_weight.astype(jnp.float32) + perturbation).astype(jnp.bfloat16)
    second = jnp.dot(
        tokens,
        lax.all_gather(own_perturbed, "dp", axis=0, tiled=True),
        preferred_element_type=jnp.float32,
    )
    second_grad = head_backward(second, upstream, norm_gain)
    sharp_grad = lax.psum_scatter(
        left_product(tokens, second_grad), "dp", scatter_dimension=0, tiled=True
    )
    return (perturbation, sharp_grad)


def cube_kernel(
    radius, n_mp,
    tok_hbm, w_hbm, gain_hbm, up_hbm,
    pert_ref, sharp_ref,
    tok_ref, gain_ref, up_ref, weight, query, near, side, turned, grads, grads2,
    part_out, part_in, moved, core_out, core_in, side_out, side_in, delta,
    sharp_out, sharp_in, total_dp, total_mp,
    load_sem, send_sem, recv_sem, hello,
):
    n_tok = tok_ref.shape[0]
    rows = pert_ref.shape[0]
    parts, head_dim = grads.shape[1], grads.shape[3]
    me = lax.axis_index("dp")
    z = lax.axis_index("mp")
    y, x, c = me // 4, (me // 2) % 2, me % 2
    oy, ox, oc = 1 - y, 1 - x, 1 - c

    def at(yy, xx, cc):
        return (yy * 2 + xx) * 2 + cc

    partner, x_peer, y_peer = at(y, x, oc), at(y, ox, c), at(oy, x, c)
    x_cross, y_cross = at(y, ox, oc), at(oy, x, oc)
    diagonal, far = at(oy, ox, c), at(oy, ox, oc)
    dp_peers = [partner, x_peer, y_peer, x_cross, y_cross, diagonal, far]
    mp_peers = [lax.rem(z + k, n_mp) for k in range(1, n_mp)]
    parity = z % 2
    z_pair = z + 1 - 2 * parity

    barrier = pltpu.get_barrier_semaphore()
    neighbours = [partner, x_peer, y_peer, x_cross, y_cross]
    for peer in neighbours:
        pl.semaphore_signal(barrier, inc=1, device_id={"dp": peer}, device_id_type=MESH)

    def signal_z(semaphore):
        @pl.when(z > 0)
        def _():
            pl.semaphore_signal(semaphore, inc=1, device_id={"mp": z - 1}, device_id_type=MESH)

        @pl.when(z < n_mp - 1)
        def _():
            pl.semaphore_signal(semaphore, inc=1, device_id={"mp": z + 1}, device_id_type=MESH)

    z_count = jnp.where(z > 0, 1, 0) + jnp.where(z < n_mp - 1, 1, 0)
    signal_z(barrier)

    gather_peer = [x_peer, y_peer]
    reduce_peer = [y_peer, x_peer]

    def columns(s, k):
        return pl.ds((2 * k + s) * head_dim, head_dim)

    def features(owner):
        return pl.ds(pl.multiple_of(owner * rows, rows), rows)

    def block(index, size):
        return pl.ds(index * size, size)

    loads = []

    def load(source, target):
        copy = pltpu.make_async_copy(source, target, load_sem.at[len(loads)])
        copy.start()
        loads.append(copy)
        return copy

    tok_load = load(tok_hbm, tok_ref)
    weight_loads = [
        load(w_hbm.at[:, block(k, 2 * head_dim)], weight.at[:, block(k, 2 * head_dim)])
        for k in range(parts)
    ]
    small_loads = [load(gain_hbm, gain_ref), load(up_hbm, up_ref)]
    near_copies = [
        load(tok_hbm.at[:, features(owner)], near.at[0, :, block(index, rows)])
        for index, owner in enumerate([y_peer, me, x_peer])
    ]

    started = []

    def send(source, target, device):
        index = len(started)
        copy = pltpu.make_async_remote_copy(
            src_ref=source, dst_ref=target,
            send_sem=send_sem.at[index], recv_sem=recv_sem.at[index],
            device_id=device, device_id_type=MESH,
        )
        copy.start()
        started.append(copy)
        return copy

    def relay(own):
        count = RELAY[own]
        return pl.ds(pl.multiple_of(parity * (n_tok - count), 16), count)

    def middle(own):
        return pl.ds(RELAY[own], n_tok - 2 * RELAY[own])

    brought = {}

    def bring(own, span, kind):
        for twin in range(2):
            cc = oc if twin else c
            for s in range(2):
                if s == 0:
                    receiver, owner = at(y, ox, cc), at(y if own else oy, ox, cc)
                else:
                    receiver, owner = at(oy, x, cc), at(oy, x if own else ox, cc)
                slot = 1 - s if own else s
                brought[s, own, twin, kind] = send(
                    tok_ref.at[span, features(owner)],
                    side.at[s, twin, span, block(slot, rows)], {"dp": receiver},
                )

    from_partner = []

    def bring_near():
        for index, owner in enumerate([at(oy, x, oc), partner, at(y, ox, oc)]):
            from_partner.append(
                send(tok_ref.at[:, features(owner)], near.at[1, :, block(index, rows)], {"dp": partner})
            )

    passed = {}

    def pass_on(own, twin):
        for s in range(2):
            brought[s, own, twin, 0].wait_recv()
            piece = side.at[s, twin, relay(own), block(1 - s if own else s, rows)]
            passed[s, own, twin] = send(piece, piece, {"mp": z_pair})

    def backward(out, s, k):
        half = n_tok // 2
        for low in (0, half):
            span = pl.ds(low, half)
            values = query[span, columns(s, k)]
            centred = values - jnp.mean(values, axis=-1, keepdims=True)
            inverse = lax.rsqrt(jnp.mean(centred * centred, axis=-1, keepdims=True) + 1e-06)
            normed = centred * inverse
            scaled = up_ref[span, columns(s, k)].astype(F32) * gain_ref[...]
            result = (
                scaled
                - jnp.mean(scaled, axis=-1, keepdims=True)
                - normed * jnp.mean(scaled * normed, axis=-1, keepdims=True)
            ) * inverse
            out[s, k, span] = result.astype(BF16)

    def spread(buffer, s, k):
        own = buffer.at[s, k, block(0, n_tok)]
        far_copy = send(own, buffer.at[s, k, block(2, n_tok)], {"dp": gather_peer[s]})
        near_copy = send(own, buffer.at[s, k, block(1, n_tok)], {"dp": partner})
        return far_copy, near_copy

    def forward(buffer, s, k, copies):
        copies[0].wait_recv()
        return send(
            buffer.at[s, k, block(2, n_tok)], buffer.at[s, k, block(3, n_tok)], {"dp": partner}
        )

    gathers = {}

    def first(k):
        weight_loads[k].wait()
        span = block(k, 2 * head_dim)
        query[:, span] = jnp.dot(tok_ref[...], weight[:, span], preferred_element_type=F32)
        if k == 0:
            for copy in small_loads:
                copy.wait()
        for s in range(2):
            backward(grads, s, k)

    tok_load.wait()
    for k in range(EARLY):
        first(k)
    pl.semaphore_wait(barrier, len(neighbours) + z_count)
    pl.semaphore_signal(hello.at[0], inc=1, device_id={"dp": y_peer}, device_id_type=MESH)
    signal_z(hello.at[1])
    for own in range(2):
        bring(own, relay(own), 0)
    for k in range(parts):
        if k >= EARLY:
            first(k)
        for s in range(2):
            gathers[s, k] = spread(grads, s, k)
        if k > 0:
            pass_on(0, k - 1)
        if k == 0:
            bring_near()
            for own in range(2):
                if 2 * RELAY[own] < n_tok:
                    bring(own, middle(own), 1)

    for copy in near_copies:
        copy.wait()

    def turn_near(which):
        for index, places in enumerate([[(0, 0)], [(0, 1), (1, 1)], [(1, 0)]]):
            value = near[which, :, block(index, rows)].T
            for s, target in places:
                turned[s, target, :, block(which, n_tok)] = value

    def turn_side(s, own):
        for twin in range(2):
            if 2 * RELAY[own] < n_tok:
                brought[s, own, twin, 1].wait_recv()
            passed[s, own, twin].wait_recv()
            slot = 1 - s if own else s
            value = side[s, twin, :, block(slot, rows)].T
            turned[s, own, :, block(2 + twin, n_tok)] = value

    for hop in range(1, n_mp - 2):
        pl.semaphore_wait(hello.at[hop], z_count)
        signal_z(hello.at[hop + 1])
    turn_near(0)
    for twin in range(2):
        pass_on(1, twin)
    for copy in from_partner:
        copy.wait_recv()
    turn_near(1)

    def product(s, k, target):
        total = None
        for slot in range(4):
            value = jnp.dot(
                turned[s, target, :, block(slot, n_tok)], grads[s, k, block(slot, n_tok)],
                preferred_element_type=F32,
            ).astype(BF16).astype(F32)
            total = value if total is None else total + value
        return total

    def gathered(copies, last):
        copies[1].wait_recv()
        last.wait_recv()

    lasts, part_copies = {}, {}
    for s in range(2):
        lasts[s, 0] = forward(grads, s, 0, gathers[s, 0])
    for s in range(2):
        turn_side(s, 0)
    for k in range(parts):
        for s in range(2):
            if k > 0:
                lasts[s, k] = forward(grads, s, k, gathers[s, k])
        for s in range(2):
            gathered(gathers[s, k], lasts[s, k])
            part_out[s, k] = product(s, k, 0).astype(BF16)
            part_copies[s, k] = send(part_out.at[s, k], part_in.at[s, k], {"dp": reduce_peer[s]})
    for s in range(2):
        turn_side(s, 1)
    moved_copies = {}

    def copy_moved(s, k):
        own, other = block(1 - s, rows), block(s, rows)
        moved_copies[s, k] = send(
            moved.at[s, k, own], moved.at[s, k, other], {"dp": reduce_peer[s]}
        )

    squares = None
    for k in range(parts):
        for s in range(2):
            value = product(s, k, 1)
            part_copies[s, k].wait_recv()
            value = value + part_in[s, k].astype(F32)
            pert_ref[:, columns(s, k)] = value
            moved[s, k, block(1 - s, rows)] = value.astype(BF16)
            square = jnp.sum((value * value).reshape(rows // 8, 8, head_dim), axis=0)
            squares = square if squares is None else squares + square
            if k + 2 < parts:
                copy_moved(s, k)
    pl.semaphore_wait(hello.at[0], 1)
    pl.semaphore_wait(hello.at[n_mp - 2], z_count)
    total_dp[me] = squares
    dp_copies = [send(total_dp.at[me], total_dp.at[me], {"dp": peer}) for peer in dp_peers]
    for k in range(parts - 2, parts):
        for s in range(2):
            copy_moved(s, k)

    def moving(s, tokens):
        if tokens < 2:
            return near[tokens, :, pl.ds(s * rows, 2 * rows)]
        return side[s, tokens - 2]

    def shift(s, k, tokens):
        return jnp.dot(moving(s, tokens), moved[s, k], preferred_element_type=F32)

    def update(s, k):
        side_copies[s, k].wait_recv()
        query[:, columns(s, k)] += (delta[s, k] + side_in[s, k].astype(F32)) * scale
        backward(grads2, s, k)
        gathers[s, k] = spread(grads2, s, k)

    core_copies, side_copies = {}, {}

    def to_partner(s, k):
        moved_copies[s, k].wait_recv()
        core_out[s, k, 0] = shift(s, k, 3).astype(BF16)
        core_out[s, k, 1] = shift(s, k, 1).astype(BF16)
        core_copies[s, k] = send(core_out.at[s, k], core_in.at[s, k], {"dp": partner})

    def to_side(s, k):
        value = shift(s, k, 2)
        core_copies[s, k].wait_recv()
        side_out[s, k] = (value + core_in[s, k, 0].astype(F32)).astype(BF16)
        side_copies[s, k] = send(side_out.at[s, k], side_in.at[s, k], {"dp": gather_peer[s]})
        delta[s, k] = shift(s, k, 0) + core_in[s, k, 1].astype(F32)

    for s in range(2):
        to_partner(s, 0)
    for copy in dp_copies:
        copy.wait_recv()
    summed = total_dp[0]
    for shard in range(1, total_dp.shape[0]):
        summed = summed + total_dp[shard]
    total_mp[z] = summed
    mp_copies = [send(total_mp.at[z], total_mp.at[z], {"mp": peer}) for peer in mp_peers]
    for s in range(2):
        to_side(s, 0)
    for k in range(1, parts - 1):
        for s in range(2):
            to_partner(s, k)
        for s in range(2):
            to_side(s, k)
    for s in range(2):
        to_partner(s, parts - 1)
    for copy in mp_copies:
        copy.wait_recv()
    summed = total_mp[0]
    for index in range(1, n_mp):
        summed = summed + total_mp[index]
    scale = radius / (jnp.sqrt(jnp.sum(summed, keepdims=True)) + 1e-12)
    for s in range(2):
        update(s, 0)
    for s in range(2):
        to_side(s, parts - 1)
    for k in range(1, parts):
        for s in range(2):
            update(s, k)
    pert_ref[...] = pert_ref[...] * scale

    sharp_copies = {}
    for k in range(parts):
        for s in range(2):
            lasts[s, k] = forward(grads2, s, k, gathers[s, k])
        for s in range(2):
            gathered(gathers[s, k], lasts[s, k])
            value = jnp.dot(turned[s, 0], grads2[s, k], preferred_element_type=F32)
            sharp_out[s, k] = value.astype(BF16)
            sharp_copies[s, k] = send(
                sharp_out.at[s, k], sharp_in.at[s, k], {"dp": reduce_peer[s]}
            )
    for k in range(parts):
        for s in range(2):
            sharp_ref[:, columns(s, k)] = jnp.dot(
                turned[s, 1], grads2[s, k], preferred_element_type=F32
            )
    for k in range(parts):
        for s in range(2):
            sharp_copies[s, k].wait_recv()
            sharp_ref[:, columns(s, k)] += sharp_in[s, k].astype(F32)
    for copy in started:
        copy.wait_send()


def cube_step(n_dp, n_mp, tokens, weight, norm_gain, upstream):
    n_tok, feat = tokens.shape
    columns = weight.shape[1]
    head_dim = norm_gain.shape[0]
    rows = feat // n_dp
    parts = columns // (2 * head_dim)
    radius = radius_coef * math.sqrt(feat * columns * n_mp)
    copies = 19 + 4 * sum(2 * count < n_tok for count in RELAY) + 2 * parts * 11 + (n_dp - 1) + (n_mp - 1)
    vmem = pl.BlockSpec(memory_space=pltpu.VMEM)
    owned = pltpu.VMEM((rows, columns), F32)
    pieces = [
        pltpu.VMEM((2, parts, rows, head_dim), BF16),
        pltpu.VMEM((2, parts, rows, head_dim), BF16),
    ]
    return pl.pallas_call(
        functools.partial(cube_kernel, radius, n_mp),
        out_shape=(owned, owned),
        in_specs=[pl.BlockSpec(memory_space=pl.ANY)] * 4,
        out_specs=(vmem, vmem),
        scratch_shapes=[
            pltpu.VMEM((n_tok, feat), BF16),
            pltpu.VMEM((1, head_dim), F32),
            pltpu.VMEM((n_tok, columns), BF16),
            pltpu.VMEM((feat, columns), BF16),
            pltpu.VMEM((n_tok, columns), F32),
            pltpu.VMEM((2, n_tok, 3 * rows), BF16),
            pltpu.VMEM((2, 2, n_tok, 2 * rows), BF16),
            pltpu.VMEM((2, 2, rows, 4 * n_tok), BF16),
            pltpu.VMEM((2, parts, 4 * n_tok, head_dim), BF16),
            pltpu.VMEM((2, parts, 4 * n_tok, head_dim), BF16),
        ]
        + pieces
        + [
            pltpu.VMEM((2, parts, 2 * rows, head_dim), BF16),
            pltpu.VMEM((2, parts, 2, n_tok, head_dim), BF16),
            pltpu.VMEM((2, parts, 2, n_tok, head_dim), BF16),
            pltpu.VMEM((2, parts, n_tok, head_dim), BF16),
            pltpu.VMEM((2, parts, n_tok, head_dim), BF16),
            pltpu.VMEM((2, parts, n_tok, head_dim), F32),
        ]
        + pieces
        + [
            pltpu.VMEM((n_dp, 8, 128), F32),
            pltpu.VMEM((n_mp, 8, 128), F32),
            pltpu.SemaphoreType.DMA((parts + 6,)),
            pltpu.SemaphoreType.DMA((copies,)),
            pltpu.SemaphoreType.DMA((copies,)),
            pltpu.SemaphoreType.REGULAR((n_mp - 1,)),
        ],
        compiler_params=pltpu.CompilerParams(
            collective_id=0, has_side_effects=True, vmem_limit_bytes=60 * 1024 * 1024
        ),
        name="cube_step",
    )(tokens, weight, norm_gain.reshape(1, -1), upstream)


def solution(mesh):
    n_dp, n_mp = mesh.shape["dp"], mesh.shape["mp"]
    step = functools.partial(cube_step, n_dp, n_mp) if n_dp == 8 and n_mp == 4 else general_step
    in_specs = (P("dp", None), P(None, "mp"), P(), P("dp", "mp"))
    out_specs = (P("dp", "mp"), P("dp", "mp"))
    return jax.shard_map(
        step, mesh=mesh, in_specs=in_specs, out_specs=out_specs, check_vma=False
    )
```
